32 devices in a mesh: mem: 4 (over y, x), lat: 8 (over z, core).
Axes of the slice: x: 2, y: 2, z: 4, core: 2. Of those that a mesh axis runs over, the one named last changes fastest.
Arguments:
- controls: float32 [24, 16, 8, 96], P('mem', None, 'lat'), may hold values from -6 to 6
- perturbations: bfloat16 [24, 64, 32, 384], P('mem', None, 'lat'), may hold values from -1.25 to 1.25
- precision_weight: bfloat16 [64, 128, 1536], P(None, 'lat'), may hold values from 0.25 to 4
- north_coef: float32 [128, 1536], P('lat'), may hold values from 0.02 to 0.24
- east_coef: float32 [128, 1536], P('lat'), may hold values from 0.02 to 0.24
- fine_source: int32 [128], P('lat'), may hold values from 0 to 30, as said below
- fine_frac: float32 [128], P('lat'), may hold values from 0 to 1
Outputs:
- gradient: float32 [24, 16, 8, 96], P('mem', None, 'lat')
The draws below stay inside these ranges and needn't reach their ends.
Inputs may be any that keep to these rules, and one draw needn't show every extreme that they name: Fine row f lies in band b = f // 16; its source rows fine_source[f] and fine_source[f] + 1 satisfy max(b * 4 - 4, 0) <= fine_source[f] <= min((b + 1) * 4 + 2, 30), and both ends are reached in every band.
All inputs are finite; a program needn't handle non-finite values.
Results may differ from the reference program's by a relative error of at most 0.0003.
Values sent between devices are 32-bit elements; how exact they have to be, the bound alone decides.
A program may use at most 128 MiB of HBM per device.

```python
import math
import jax
import jax.numpy as jnp
from jax import lax

CLEV = 16
CLON = 96
PASSES = 5
REACH = 4
MEMBERS = 24
LEV = 64
CLAT = 8
MROWS = 4
FROWS = 16
MLAT = 32
FLAT = 128
MLON = 384
FLON = 1536


def draw_fine_source(key, part):
    rows_all = jnp.arange(FLAT, dtype=jnp.int32)
    band = rows_all // FROWS
    within = rows_all % FROWS
    start = band * MROWS
    lowest = jnp.maximum(start - REACH, 0)
    highest = jnp.minimum(start + MROWS + REACH - 2, MLAT - 2)
    base = start + within * MROWS // FROWS
    jitter = jax.random.randint(key, (FLAT,), -REACH, REACH + 1, dtype=jnp.int32)
    source = jnp.clip(base + jitter, lowest, highest)
    source = jnp.where(within == 0, lowest, source)
    source = jnp.where(within == FROWS - 1, highest, source)
    return source.astype(jnp.int32)


def steps_of(own_key, extent, cuts, smallest, largest):
    def one(dim, blocks):
        draws = jax.random.uniform(jax.random.fold_in(jax.random.fold_in(own_key, 6), dim), (blocks,), jnp.float32, smallest / len(cuts), largest / len(cuts))
        return jnp.repeat(jnp.exp(draws), extent[dim] // blocks).reshape((-1,) + (1,) * (len(extent) - dim - 1))

    level = one(*cuts[0])
    for cut in cuts[1:]:
        level = level * one(*cut)
    return level


def centred(key, extent, width, limit, pieces=(), kind=jnp.bfloat16):
    gain = steps_of(key, extent, pieces, -0.22, 0.18) if pieces else 1.0
    values = jax.random.normal(key, extent, jnp.float32) * width * gain
    return jnp.minimum(jnp.maximum(values, -limit), limit).astype(kind)


def setup_inputs(seed: int = 0) -> dict:
    splits = jax.random.split(jax.random.key(seed), 8)
    controls = centred(splits[0], (MEMBERS, CLEV, CLAT, CLON), 1.0, 6.0, ((0, 4), (2, 8)), jnp.float32)
    perturbations = centred(splits[1], (MEMBERS, LEV, MLAT, MLON), MEMBERS ** -0.5, 1.25, ((0, 4), (2, 8)))
    precision_weight = jnp.clip(jnp.exp(math.log(4.0) - 2.7725887 * jax.random.uniform(splits[2], (LEV, FLAT, FLON), jnp.float32) ** steps_of(splits[2], (LEV, FLAT, FLON), ((1, 8),), -0.2, 0.2)), 0.25, 4.0).astype(jnp.bfloat16)
    north_coef = jnp.clip(0.02 + 0.22 * jax.random.uniform(splits[3], (FLAT, FLON), jnp.float32) ** steps_of(splits[3], (FLAT, FLON), ((0, 8),), -0.2, 0.2), 0.02, 0.24)
    east_coef = jnp.clip(0.02 + 0.22 * jax.random.uniform(splits[4], (FLAT, FLON), jnp.float32) ** steps_of(splits[4], (FLAT, FLON), ((0, 8),), -0.2, 0.2), 0.02, 0.24)
    fine_source = draw_fine_source(jax.random.fold_in(splits[7], 71), 0)
    fine_frac = jnp.clip(1.0 * jax.random.uniform(splits[6], (FLAT,), jnp.float32) ** steps_of(splits[6], (FLAT,), ((0, 8),), -0.2, 0.2), 0.0, 1.0)
    return dict(controls=controls, perturbations=perturbations, precision_weight=precision_weight, north_coef=north_coef, east_coef=east_coef, fine_source=fine_source, fine_frac=fine_frac)


def refine(padded, dimension):
    count = padded.shape[dimension] - 2
    previous = lax.slice_in_dim(padded, 0, count, axis=dimension)
    current = lax.slice_in_dim(padded, 1, count + 1, axis=dimension)
    following = lax.slice_in_dim(padded, 2, count + 2, axis=dimension)
    phases = [0.375 * previous + 0.625 * current, 0.125 * previous + 0.875 * current, 0.875 * current + 0.125 * following, 0.625 * current + 0.375 * following]
    stacked = jnp.stack(phases, axis=dimension + 1)
    new_shape = list(padded.shape)
    new_shape[dimension] = 4 * count
    return stacked.reshape(new_shape)

def raise_padded(padded):
    field = refine(jnp.pad(padded, ((0, 0), (1, 1), (0, 0), (0, 0)), mode='edge'), 1)
    field = refine(jnp.pad(field, ((0, 0), (0, 0), (0, 0), (1, 1)), mode='wrap'), 3)
    return refine(field, 2)

def diffuse(padded, north_pad, east_rows):
    center = padded[:, 1:-1]
    upward = north_pad[1:-1] * (padded[:, 2:] - center)
    downward = north_pad[:-2] * (padded[:, :-2] - center)
    eastward = east_rows * (jnp.roll(center, -1, 2) - center)
    westward = jnp.roll(east_rows, 1, 1) * (jnp.roll(center, 1, 2) - center)
    return center + upward + downward + eastward + westward

def to_fine(increment, fine_source, fine_frac):
    lower_rows = jnp.take(increment, fine_source, axis=1)
    upper_rows = jnp.take(increment, fine_source + 1, axis=1)
    fraction = fine_frac[:, None]
    blended = (1.0 - fraction) * lower_rows + fraction * upper_rows
    return refine(jnp.pad(blended, ((0, 0), (0, 0), (1, 1)), mode='wrap'), 2)

def reference(controls, perturbations, precision_weight, north_coef, east_coef, fine_source, fine_frac):

    def raise_one(member_control):
        padded = jnp.pad(member_control[None], ((0, 0), (0, 0), (1, 1), (0, 0)), mode='edge')
        return raise_padded(padded)[0]

    def accumulate(running, member_pair):
        return (running + member_pair[1].astype(jnp.float32) * raise_one(member_pair[0]), None)
    start_sum = jnp.zeros((LEV, MLAT, MLON), jnp.float32)
    increment, _ = lax.scan(accumulate, start_sum, (controls, perturbations))
    fine_grid, pull_fine = jax.vjp(lambda field: to_fine(field, fine_source, fine_frac), increment)
    zero_row = jnp.zeros((1, FLON), jnp.float32)
    north_pad = jnp.concatenate([zero_row, north_coef, zero_row], axis=0)

    def smooth(field):
        for repeat in range(PASSES):
            field = diffuse(jnp.pad(field, ((0, 0), (1, 1), (0, 0))), north_pad, east_coef)
        return field
    weighted = precision_weight.astype(jnp.float32) * smooth(fine_grid)
    fine_adjoint = pull_fine(smooth(weighted))[0]

    def adjoint_one(member_pair):
        _, pull_back = jax.vjp(raise_one, member_pair[0])
        return pull_back(member_pair[1].astype(jnp.float32) * fine_adjoint)[0]
    adjoints = lax.map(adjoint_one, (controls, perturbations))
    return controls + adjoints
```

```python
import functools
import jax
import jax.numpy as jnp
import numpy as np
from jax import lax
from jax.experimental import pallas as pl
from jax.experimental.pallas import tpu as pltpu
from jax.sharding import PartitionSpec as P

PASSES = 5
REACH = 4
LANES = 128
F32 = jnp.float32
BF16 = jnp.bfloat16
MESH = pl.DeviceIdType.MESH


def refine_matrix(count, mode):
    weights = [(0.375, 0.625, 0.0), (0.125, 0.875, 0.0), (0.0, 0.875, 0.125), (0.0, 0.625, 0.375)]
    full = np.zeros((4 * count, count + 2), np.float32)
    for q in range(count):
        for r in range(4):
            full[4 * q + r, q : q + 3] += weights[r]
    if mode == "pad":
        return full
    inner = full[:, 1:-1].copy()
    if mode == "edge":
        inner[:, 0] += full[:, 0]
        inner[:, -1] += full[:, -1]
    else:
        inner[:, -1] += full[:, 0]
        inner[:, 0] += full[:, -1]
    return inner


def split3(value):
    high = value.astype(BF16)
    rest = value - high.astype(F32)
    mid = rest.astype(BF16)
    low = (rest - mid.astype(F32)).astype(BF16)
    return high, mid, low


def dot(a, b):
    return jnp.dot(a, b, preferred_element_type=F32)


def kernel(
    dims,
    ctl_ref, pert_hbm, pw_hbm, north_ref, east_ref, sf_ref, up_ref, lon_ref, down_ref, lont_ref,
    out_ref,
    ctl, pert, pw, wrows, co, sfr, ls, mids, rsr, midx, fld, blend, contrib, adjr, fa, gp, gpr, wown,
    local_sem, send_sem, recv_sem,
):
    nm, nl, mb, cl, cw, lv, mr, mw, fr, fw = dims
    lp = lv // nm
    h1, h2 = 2 * PASSES, PASSES
    ext = fr + 2 * h1
    mem, lat = lax.axis_index("mem"), lax.axis_index("lat")
    first, last = lat == 0, lat == nl - 1
    blocks = lp // 8

    cp_pert = pltpu.make_async_copy(pert_hbm, pert, local_sem.at[0])
    cp_pert.start()
    cp_pw = pltpu.make_async_copy(
        pw_hbm.at[pl.ds(mem * lp, lp)], pw, local_sem.at[1]
    )
    cp_pw.start()

    barrier = pltpu.get_barrier_semaphore()
    for step in (1, 2):
        @pl.when(lat >= step)
        def _():
            pl.semaphore_signal(barrier, inc=1, device_id={"lat": lat - step}, device_id_type=MESH)

        @pl.when(lat < nl - step)
        def _():
            pl.semaphore_signal(barrier, inc=1, device_id={"lat": lat + step}, device_id_type=MESH)
    for k in range(1, nm):
        pl.semaphore_signal(
            barrier, inc=1, device_id={"mem": lax.rem(mem + k, nm)}, device_id_type=MESH
        )
    present = nm - 1
    for step in (1, 2):
        present = present + (lat >= step).astype(jnp.int32) + (lat < nl - step).astype(jnp.int32)
    pl.semaphore_wait(barrier, present)

    def lat_copy(slot, step, src, dst):
        copy = pltpu.make_async_remote_copy(
            src_ref=src, dst_ref=dst, send_sem=send_sem.at[slot], recv_sem=recv_sem.at[slot],
            device_id={"lat": lat + step}, device_id_type=MESH,
        )
        if step > 0:
            return copy, lat < nl - step, lat >= step
        return copy, lat >= -step, lat < nl + step

    def start(item):
        copy, sends, _ = item

        @pl.when(sends)
        def _():
            copy.start()

    def wait_recv(item):
        copy, _, receives = item

        @pl.when(receives)
        def _():
            copy.wait_recv()

    def wait_send(item):
        copy, sends, _ = item

        @pl.when(sends)
        def _():
            copy.wait_send()

    pending = []

    c_up = lat_copy(0, 1, ctl_ref, ctl.at[0])
    c_dn = lat_copy(1, -1, ctl_ref, ctl.at[1])
    s_up = lat_copy(2, 1, sf_ref.at[pl.ds(fr - h1, h1)], sfr.at[pl.ds(0, h1)])
    s_dn = lat_copy(3, -1, sf_ref.at[pl.ds(0, h1)], sfr.at[pl.ds(h1, h1)])
    for item in (c_up, c_dn, s_up, s_dn):
        start(item)
        pending.append(item)

    rows_i = lax.broadcasted_iota(jnp.int32, (4 * LANES, 4 * LANES), 0)
    cols_i = lax.broadcasted_iota(jnp.int32, (4 * LANES, 4 * LANES), 1)
    perm = (rows_i == 4 * lax.rem(cols_i, LANES) + lax.div(cols_i, LANES)).astype(F32).astype(BF16)
    qblocks = mw // LANES

    for kind, ref in enumerate((north_ref, east_ref)):
        stacked = jnp.concatenate(split3(ref[...]), axis=0)
        for block in range(qblocks):
            moved = dot(stacked[:, block * 4 * LANES : (block + 1) * 4 * LANES], perm)
            exact = (moved[:fr] + moved[fr : 2 * fr]) + moved[2 * fr :]
            for phase in range(4):
                lanes = pl.ds(phase * mw + block * LANES, LANES)
                for row in range(fr):
                    co[h1 + row, kind : kind + 1, lanes] = exact[
                        row : row + 1, phase * LANES : (phase + 1) * LANES
                    ]
    k_up = lat_copy(4, 1, co.at[pl.ds(fr, h1)], co.at[pl.ds(0, h1)])
    k_dn = lat_copy(5, -1, co.at[pl.ds(h1, h1)], co.at[pl.ds(h1 + fr, h1)])
    for item in (k_up, k_dn):
        start(item)
        pending.append(item)

    wait_recv(c_up)
    wait_recv(c_dn)
    own = ctl_ref[...]
    below = jnp.where(first, own, ctl[0])
    above = jnp.where(last, own, ctl[1])
    lon = lon_ref[...]
    wide = []
    for part in (below, own, above):
        parts = split3(part.reshape(mb * cl, cw))
        wide.append(dot(parts[0], lon) + (dot(parts[1], lon) + dot(parts[2], lon)))
    cp_pert.wait()
    up3 = up_ref[...]
    for m in range(mb):
        stack = jnp.concatenate([w[m * cl : (m + 1) * cl] for w in wide], axis=0)
        raised = dot(up3, jnp.concatenate(split3(stack), axis=0))
        term = pert[m].astype(F32) * raised
        for t in range(qblocks):
            piece = term[:, t * LANES : (t + 1) * LANES]
            if m == 0:
                ls[t] = piece
            else:
                ls[t] += piece
    for r in range(mr):
        for t in range(qblocks):
            mids[r, :, t * LANES : (t + 1) * LANES] = ls[t, pl.ds(r, lv, stride=mr), :]

    rs = []
    for k in range(1, nm):
        target = lax.rem(mem + k, nm)
        copy = pltpu.make_async_remote_copy(
            src_ref=mids.at[:, pl.ds(pl.multiple_of(target * lp, 8), lp), :],
            dst_ref=rsr.at[k - 1],
            send_sem=send_sem.at[16 + k], recv_sem=recv_sem.at[16 + k],
            device_id={"mem": target}, device_id_type=MESH,
        )
        copy.start()
        rs.append(copy)

    cp_pw.wait()
    count = lp * fr
    to_i = lax.broadcasted_iota(jnp.int32, (count, count), 0)
    from_i = lax.broadcasted_iota(jnp.int32, (count, count), 1)
    turn = (from_i == lax.rem(to_i, lp) * fr + lax.div(to_i, lp)).astype(F32).astype(BF16)
    for block in range(qblocks):
        piece = pw[:, :, block * 4 * LANES : (block + 1) * 4 * LANES].reshape(count, 4 * LANES)
        turned = dot(turn, piece).astype(BF16)
        moved = dot(turned, perm)
        for phase in range(4):
            lanes = pl.ds(phase * mw + block * LANES, LANES)
            wown[:, :, lanes] = moved[:, phase * LANES : (phase + 1) * LANES].reshape(fr, lp, LANES)
    w_up = lat_copy(6, 1, wown.at[pl.ds(fr - h2, h2)], wrows.at[0])
    w_dn = lat_copy(7, -1, wown.at[pl.ds(0, h2)], wrows.at[1])
    for item in (w_up, w_dn):
        pending.append(item)

    mine = pl.ds(pl.multiple_of(mem * lp, 8), lp)
    total = mids[:, mine, :]
    for k in range(1, nm):
        rs[k - 1].wait_recv()
        total = total + rsr[k - 1]
    centre = 2 * mr
    midx[pl.ds(centre, mr)] = total
    near = []
    for slot, step in ((8, 1), (9, -1), (10, 2), (11, -2)):
        item = lat_copy(
            slot, step, midx.at[pl.ds(centre, mr)], midx.at[pl.ds(centre - step * mr, mr)]
        )
        start(item)
        pending.append(item)
        near.append(item)
    start(w_up)
    start(w_dn)

    zero_mid = jnp.zeros((mr, lp, mw), F32)
    for at, absent in ((1, first), (0, lat < 2), (3, last), (4, lat >= nl - 2)):
        @pl.when(absent)
        def _():
            midx[pl.ds(at * mr, mr)] = zero_mid

    @pl.when(first)
    def _():
        fld[h1 - 1] = jnp.zeros((lp, fw), F32)
        co[h1 - 1] = jnp.zeros((2, fw), F32)

    @pl.when(last)
    def _():
        fld[h1 + fr] = jnp.zeros((lp, fw), F32)

    for item in (s_up, s_dn, *near, k_up, k_dn):
        wait_recv(item)

    origin = (lat * mr - 2 * mr).astype(F32)

    def weight_of(source, fraction, r):
        place = source - origin
        lower = jnp.where(place == float(r), 1.0 - fraction, 0.0)
        return lower + jnp.where(place == float(r - 1), fraction, 0.0)

    def make_rows(ref, ref_row, ext_row, rows, base):
        def step(i, carry):
            source = jnp.broadcast_to(ref[ref_row + i, 0:1, :], (8, LANES))
            fraction = jnp.broadcast_to(ref[ref_row + i, 1:2, :], (8, LANES))
            weights = [weight_of(source, fraction, base + r) for r in range(3 * mr)]
            for b in range(blocks):
                levels = slice(8 * b, 8 * b + 8)
                pieces = []
                for t in range(qblocks):
                    value = weights[0] * midx[base, levels, t * LANES : (t + 1) * LANES]
                    for r in range(1, 3 * mr):
                        value = value + weights[r] * midx[
                            base + r, levels, t * LANES : (t + 1) * LANES
                        ]
                    pieces.append(value)
                row = jnp.concatenate(pieces, axis=1)
                before = pltpu.roll(row, 1, 1)
                after = pltpu.roll(row, mw - 1, 1)
                at = ext_row + i
                fld[at, levels, 0:mw] = 0.375 * before + 0.625 * row
                fld[at, levels, mw : 2 * mw] = 0.125 * before + 0.875 * row
                fld[at, levels, 2 * mw : 3 * mw] = 0.875 * row + 0.125 * after
                fld[at, levels, 3 * mw : 4 * mw] = 0.625 * row + 0.375 * after
            return carry

        lax.fori_loop(0, rows, step, 0)

    make_rows(sf_ref, 0, h1, fr, mr)

    @pl.when(jnp.logical_not(first))
    def _():
        make_rows(sfr, 0, 0, h1, 0)

    @pl.when(jnp.logical_not(last))
    def _():
        make_rows(sfr, h1, h1 + fr, h1, 2 * mr)

    def one_pass(low, high):
        for b in range(blocks):
            levels = slice(8 * b, 8 * b + 8)

            def phases(row):
                return [fld[row, levels, p * mw : (p + 1) * mw] for p in range(4)]

            def coef(row, kind, p):
                return co[row, kind : kind + 1, p * mw : (p + 1) * mw]

            centre0 = phases(low)
            under = phases(low - 1)
            flux0 = [coef(low - 1, 0, p) * (centre0[p] - under[p]) for p in range(4)]

            def step(row, carry):
                now, below_flux = carry
                over = phases(row + 1)
                east = [coef(row, 1, p) * (now[p + 1] - now[p]) for p in range(3)]
                east.append(coef(row, 1, 3) * (pltpu.roll(now[0], mw - 1, 1) - now[3]))
                west = [pltpu.roll(east[3], 1, 1)] + east[:3]
                north = [coef(row, 0, p) * (over[p] - now[p]) for p in range(4)]
                for p in range(4):
                    fld[row, levels, p * mw : (p + 1) * mw] = now[p] + (
                        (north[p] - below_flux[p]) + (east[p] - west[p])
                    )
                return over, north

            lax.fori_loop(low, high, step, (centre0, flux0))

    def smooth(margin):
        def body(p, carry):
            low = jnp.where(first, h1, margin + 1 + p)
            high = jnp.where(last, h1 + fr, ext - margin - 1 - p)
            one_pass(low, high)
            return carry

        lax.fori_loop(0, PASSES, body, 0)

    smooth(0)
    wait_recv(w_up)
    wait_recv(w_dn)

    def apply_own(i, carry):
        fld[h1 + i] = fld[h1 + i] * wown[i]
        return carry

    lax.fori_loop(0, fr, apply_own, 0)

    @pl.when(jnp.logical_not(first))
    def _():
        for i in range(h2):
            fld[h1 - h2 + i] = fld[h1 - h2 + i] * wrows[0, i]

    @pl.when(jnp.logical_not(last))
    def _():
        for i in range(h2):
            fld[h1 + fr + i] = fld[h1 + fr + i] * wrows[1, i]

    smooth(PASSES)

    def narrow(i, carry):
        for b in range(blocks):
            levels = slice(8 * b, 8 * b + 8)
            g = [fld[h1 + i, levels, p * mw : (p + 1) * mw] for p in range(4)]
            value = 0.625 * (g[0] + g[3]) + 0.875 * (g[1] + g[2])
            value = value + pltpu.roll(0.375 * g[0] + 0.125 * g[1], mw - 1, 1)
            blend[i, levels, :] = value + pltpu.roll(0.125 * g[2] + 0.375 * g[3], 1, 1)
        return carry

    lax.fori_loop(0, fr, narrow, 0)

    def gather(r, carry):
        weights = []
        place_of = (r + mr).astype(F32)
        for f in range(fr):
            source = jnp.broadcast_to(sf_ref[f, 0:1, :], (8, LANES)) - origin
            fraction = jnp.broadcast_to(sf_ref[f, 1:2, :], (8, LANES))
            lower = jnp.where(source == place_of, 1.0 - fraction, 0.0)
            weights.append(lower + jnp.where(source == place_of - 1.0, fraction, 0.0))
        for b in range(blocks):
            levels = slice(8 * b, 8 * b + 8)
            for t in range(qblocks):
                lanes = slice(t * LANES, (t + 1) * LANES)
                value = weights[0] * blend[0, levels, lanes]
                for f in range(1, fr):
                    value = value + weights[f] * blend[f, levels, lanes]
                contrib[r, levels, lanes] = value
        return carry

    lax.fori_loop(0, 3 * mr, gather, 0)
    a_up = lat_copy(12, 1, contrib.at[pl.ds(2 * mr, mr)], adjr.at[0])
    a_dn = lat_copy(13, -1, contrib.at[pl.ds(0, mr)], adjr.at[1])
    for item in (a_up, a_dn):
        start(item)
        pending.append(item)
    for at, absent in ((0, first), (1, last)):
        @pl.when(absent)
        def _():
            adjr[at] = zero_mid
    wait_recv(a_up)
    wait_recv(a_dn)
    fa[:, mine, :] = contrib[pl.ds(mr, mr)] + (adjr[0] + adjr[1])

    ag = []
    for k in range(1, nm):
        target = lax.rem(mem + k, nm)
        copy = pltpu.make_async_remote_copy(
            src_ref=fa.at[:, mine, :], dst_ref=fa.at[:, mine, :],
            send_sem=send_sem.at[16 + nm + k], recv_sem=recv_sem.at[16 + nm + k],
            device_id={"mem": target}, device_id_type=MESH,
        )
        copy.start()
        ag.append(copy)
    for k in range(1, nm):
        ag[k - 1].wait_recv()
    for copy in rs:
        copy.wait_send()
    for r in range(mr):
        for t in range(qblocks):
            ls[t, pl.ds(r, lv, stride=mr), :] = fa[r, :, t * LANES : (t + 1) * LANES]
    spread = jnp.concatenate([ls[t] for t in range(qblocks)], axis=1)

    down = down_ref[...]
    lont = lont_ref[...]
    for m in range(mb):
        parts = split3(pert[m].astype(F32) * spread)
        tall = dot(down, parts[0]) + (dot(down, parts[1]) + dot(down, parts[2]))
        thin = split3(tall)
        grad = dot(thin[0], lont) + (dot(thin[1], lont) + dot(thin[2], lont))
        for c in range(3):
            gp[c, m] = grad[c * cl : (c + 1) * cl]
    g_up = lat_copy(14, 1, gp.at[2], gpr.at[0])
    g_dn = lat_copy(15, -1, gp.at[0], gpr.at[1])
    for item in (g_up, g_dn):
        start(item)
        pending.append(item)

    @pl.when(first)
    def _():
        gpr[0] = gp[0]

    @pl.when(last)
    def _():
        gpr[1] = gp[2]

    wait_recv(g_up)
    wait_recv(g_dn)
    out_ref[...] = ctl_ref[...] + (gp[1] + (gpr[0] + gpr[1]))
    for item in pending:
        wait_send(item)
    for copy in ag:
        copy.wait_send()


def body(controls, perturbations, precision_weight, north_coef, east_coef, fine_source, fine_frac):
    nm, nl = lax.axis_size("mem"), lax.axis_size("lat")
    mb, cl, _, cw = controls.shape
    _, lv, mr, mw = perturbations.shape
    fr, fw = north_coef.shape
    lp = lv // nm
    h1, h2 = 2 * PASSES, PASSES
    ext = fr + 2 * h1
    level = refine_matrix(cl, "edge")
    across = refine_matrix(1, "pad")
    up = np.einsum("vc,ra->vrac", level, across).reshape(lv * mr, 3 * cl)
    lon = refine_matrix(cw, "wrap").T
    sf = jnp.stack([fine_source.astype(F32), fine_frac], axis=1)
    sf = jnp.broadcast_to(sf[:, :, None], (fr, 2, LANES))
    vmem = pl.BlockSpec(memory_space=pltpu.VMEM)
    anywhere = pl.BlockSpec(memory_space=pl.ANY)
    dims = (nm, nl, mb, cl, cw, lv, mr, mw, fr, fw)
    slots = 17 + 2 * nm
    result = pl.pallas_call(
        functools.partial(kernel, dims),
        out_shape=jax.ShapeDtypeStruct((mb, cl, cw), F32),
        in_specs=[vmem, anywhere, anywhere] + [vmem] * 7,
        out_specs=vmem,
        scratch_shapes=[
            pltpu.VMEM((2, mb, cl, cw), F32),
            pltpu.VMEM((mb, lv * mr, mw), BF16),
            pltpu.VMEM((lp, fr, fw), BF16),
            pltpu.VMEM((2, h2, lp, fw), F32),
            pltpu.VMEM((ext, 2, fw), F32),
            pltpu.VMEM((2 * h1, 2, LANES), F32),
            pltpu.VMEM((mw // LANES, lv * mr, LANES), F32),
            pltpu.VMEM((mr, lv, mw), F32),
            pltpu.VMEM((nm - 1, mr, lp, mw), F32),
            pltpu.VMEM((5 * mr, lp, mw), F32),
            pltpu.VMEM((ext, lp, fw), F32),
            pltpu.VMEM((fr, lp, mw), F32),
            pltpu.VMEM((3 * mr, lp, mw), F32),
            pltpu.VMEM((2, mr, lp, mw), F32),
            pltpu.VMEM((mr, lv, mw), F32),
            pltpu.VMEM((3, mb, cl, cw), F32),
            pltpu.VMEM((2, mb, cl, cw), F32),
            pltpu.VMEM((fr, lp, fw), F32),
            pltpu.SemaphoreType.DMA((2,)),
            pltpu.SemaphoreType.DMA((slots,)),
            pltpu.SemaphoreType.DMA((slots,)),
        ],
        compiler_params=pltpu.CompilerParams(collective_id=0, has_side_effects=True),
    )(
        controls.reshape(mb, cl, cw),
        perturbations.reshape(mb, lv * mr, mw),
        precision_weight,
        north_coef,
        east_coef,
        sf,
        jnp.asarray(np.concatenate([up] * 3, axis=1), BF16),
        jnp.asarray(lon, BF16),
        jnp.asarray(up.T, BF16),
        jnp.asarray(lon.T, BF16),
    )
    return result.reshape(controls.shape)


def solution(mesh):
    in_specs = (
        P("mem", None, "lat", None),
        P("mem", None, "lat", None),
        P(None, "lat", None),
        P("lat", None),
        P("lat", None),
        P("lat"),
        P("lat"),
    )
    out_specs = P("mem", None, "lat", None)
    return jax.shard_map(body, mesh=mesh, in_specs=in_specs, out_specs=out_specs, check_vma=False)
```

```python
import functools
import jax
import jax.numpy as jnp
import numpy as np
from jax import lax
from jax.experimental import pallas as pl
from jax.experimental.pallas import tpu as pltpu
from jax.sharding import PartitionSpec as P

PASSES = 5
REACH = 4
LANES = 128
UNROLL = 8
F32 = jnp.float32
BF16 = jnp.bfloat16
MESH = pl.DeviceIdType.MESH


def refine_matrix(count, mode):
    weights = [(0.375, 0.625, 0.0), (0.125, 0.875, 0.0), (0.0, 0.875, 0.125), (0.0, 0.625, 0.375)]
    full = np.zeros((4 * count, count + 2), np.float32)
    for q in range(count):
        for r in range(4):
            full[4 * q + r, q : q + 3] += weights[r]
    if mode == "pad":
        return full
    inner = full[:, 1:-1].copy()
    if mode == "edge":
        inner[:, 0] += full[:, 0]
        inner[:, -1] += full[:, -1]
    else:
        inner[:, -1] += full[:, 0]
        inner[:, 0] += full[:, -1]
    return inner


def split3(value):
    high = value.astype(BF16)
    rest = value - high.astype(F32)
    mid = rest.astype(BF16)
    low = (rest - mid.astype(F32)).astype(BF16)
    return high, mid, low


def dot(a, b):
    return jnp.dot(a, b, preferred_element_type=F32)


def kernel(
    dims,
    ctl_ref, pert_hbm, pw_hbm, north_ref, east_ref, sf_ref, up_ref, lon_ref, down_ref, lont_ref,
    out_ref,
    ctl, pert, pw, wrows, co, sfr, ls, mids, rsr, midx, fld, blend, contrib, adjr, fa, gp, gpr, wown,
    local_sem, send_sem, recv_sem,
):
    nm, nl, mb, cl, cw, lv, mr, mw, fr, fw = dims
    lp = lv // nm
    h1, h2 = 2 * PASSES, PASSES
    ext = fr + 2 * h1
    mem, lat = lax.axis_index("mem"), lax.axis_index("lat")
    first, last = lat == 0, lat == nl - 1
    blocks = lp // 8

    cp_pert = pltpu.make_async_copy(pert_hbm, pert, local_sem.at[0])
    cp_pert.start()
    cp_pw = pltpu.make_async_copy(
        pw_hbm.at[pl.ds(mem * lp, lp)], pw, local_sem.at[1]
    )
    cp_pw.start()

    barrier = pltpu.get_barrier_semaphore()
    for step in (1, 2):
        @pl.when(lat >= step)
        def _():
            pl.semaphore_signal(barrier, inc=1, device_id={"lat": lat - step}, device_id_type=MESH)

        @pl.when(lat < nl - step)
        def _():
            pl.semaphore_signal(barrier, inc=1, device_id={"lat": lat + step}, device_id_type=MESH)
    for k in range(1, nm):
        pl.semaphore_signal(
            barrier, inc=1, device_id={"mem": lax.rem(mem + k, nm)}, device_id_type=MESH
        )
    present = nm - 1
    for step in (1, 2):
        present = present + (lat >= step).astype(jnp.int32) + (lat < nl - step).astype(jnp.int32)
    pl.semaphore_wait(barrier, present)

    def lat_copy(slot, step, src, dst):
        copy = pltpu.make_async_remote_copy(
            src_ref=src, dst_ref=dst, send_sem=send_sem.at[slot], recv_sem=recv_sem.at[slot],
            device_id={"lat": lat + step}, device_id_type=MESH,
        )
        if step > 0:
            return copy, lat < nl - step, lat >= step
        return copy, lat >= -step, lat < nl + step

    def start(item):
        copy, sends, _ = item

        @pl.when(sends)
        def _():
            copy.start()

    def wait_recv(item):
        copy, _, receives = item

        @pl.when(receives)
        def _():
            copy.wait_recv()

    def wait_send(item):
        copy, sends, _ = item

        @pl.when(sends)
        def _():
            copy.wait_send()

    pending = []

    c_up = lat_copy(0, 1, ctl_ref, ctl.at[0])
    c_dn = lat_copy(1, -1, ctl_ref, ctl.at[1])
    s_up = lat_copy(2, 1, sf_ref.at[pl.ds(fr - h1, h1)], sfr.at[pl.ds(0, h1)])
    s_dn = lat_copy(3, -1, sf_ref.at[pl.ds(0, h1)], sfr.at[pl.ds(h1, h1)])
    for item in (c_up, c_dn, s_up, s_dn):
        start(item)
        pending.append(item)

    rows_i = lax.broadcasted_iota(jnp.int32, (4 * LANES, 4 * LANES), 0)
    cols_i = lax.broadcasted_iota(jnp.int32, (4 * LANES, 4 * LANES), 1)
    perm = (rows_i == 4 * lax.rem(cols_i, LANES) + lax.div(cols_i, LANES)).astype(F32).astype(BF16)
    qblocks = mw // LANES

    for kind, ref in enumerate((north_ref, east_ref)):
        stacked = jnp.concatenate(split3(ref[...]), axis=0)
        edges = []
        for block in range(qblocks):
            moved = dot(stacked[:, block * 4 * LANES : (block + 1) * 4 * LANES], perm)
            exact = (moved[:fr] + moved[fr : 2 * fr]) + moved[2 * fr :]
            edges.append(exact[:, 3 * LANES :])
            for phase in range(4):
                lanes = pl.ds(phase * mw + block * LANES, LANES)
                for row in range(fr):
                    co[h1 + row, kind : kind + 1, lanes] = exact[
                        row : row + 1, phase * LANES : (phase + 1) * LANES
                    ]
    edge = pltpu.roll(jnp.concatenate(edges, axis=1), 1, 1)
    for row in range(fr):
        co[h1 + row, 2:3, 0:mw] = edge[row : row + 1]
        co[h1 + row, 2:3, mw:fw] = jnp.zeros((1, fw - mw), F32)
    k_up = lat_copy(4, 1, co.at[pl.ds(fr, h1)], co.at[pl.ds(0, h1)])
    k_dn = lat_copy(5, -1, co.at[pl.ds(h1, h1)], co.at[pl.ds(h1 + fr, h1)])
    for item in (k_up, k_dn):
        start(item)
        pending.append(item)

    wait_recv(c_up)
    wait_recv(c_dn)
    own = ctl_ref[...]
    below = jnp.where(first, own, ctl[0])
    above = jnp.where(last, own, ctl[1])
    lon = lon_ref[...]
    wide = []
    for part in (below, own, above):
        parts = split3(part.reshape(mb * cl, cw))
        wide.append(dot(parts[0], lon) + (dot(parts[1], lon) + dot(parts[2], lon)))
    cp_pert.wait()
    up3 = up_ref[...]
    for m in range(mb):
        stack = jnp.concatenate([w[m * cl : (m + 1) * cl] for w in wide], axis=0)
        raised = dot(up3, jnp.concatenate(split3(stack), axis=0))
        term = pert[m].astype(F32) * raised
        for t in range(qblocks):
            piece = term[:, t * LANES : (t + 1) * LANES]
            if m == 0:
                ls[t] = piece
            else:
                ls[t] += piece
    for r in range(mr):
        for t in range(qblocks):
            mids[r, :, t * LANES : (t + 1) * LANES] = ls[t, pl.ds(r, lv, stride=mr), :]

    rs = []
    for k in range(1, nm):
        target = lax.rem(mem + k, nm)
        copy = pltpu.make_async_remote_copy(
            src_ref=mids.at[:, pl.ds(pl.multiple_of(target * lp, 8), lp), :],
            dst_ref=rsr.at[k - 1],
            send_sem=send_sem.at[16 + k], recv_sem=recv_sem.at[16 + k],
            device_id={"mem": target}, device_id_type=MESH,
        )
        copy.start()
        rs.append(copy)

    cp_pw.wait()
    count = lp * fr
    to_i = lax.broadcasted_iota(jnp.int32, (count, count), 0)
    from_i = lax.broadcasted_iota(jnp.int32, (count, count), 1)
    turn = (from_i == lax.rem(to_i, lp) * fr + lax.div(to_i, lp)).astype(F32).astype(BF16)
    for block in range(qblocks):
        piece = pw[:, :, block * 4 * LANES : (block + 1) * 4 * LANES].reshape(count, 4 * LANES)
        turned = dot(turn, piece).astype(BF16)
        moved = dot(turned, perm)
        for phase in range(4):
            lanes = pl.ds(phase * mw + block * LANES, LANES)
            wown[:, :, lanes] = moved[:, phase * LANES : (phase + 1) * LANES].reshape(fr, lp, LANES)
    w_up = lat_copy(6, 1, wown.at[pl.ds(fr - h2, h2)], wrows.at[0])
    w_dn = lat_copy(7, -1, wown.at[pl.ds(0, h2)], wrows.at[1])
    for item in (w_up, w_dn):
        pending.append(item)

    mine = pl.ds(pl.multiple_of(mem * lp, 8), lp)
    total = mids[:, mine, :]
    for k in range(1, nm):
        rs[k - 1].wait_recv()
        total = total + rsr[k - 1]
    centre = 2 * mr
    midx[pl.ds(centre, mr)] = total
    near = []
    for slot, step in ((8, 1), (9, -1), (10, 2), (11, -2)):
        item = lat_copy(
            slot, step, midx.at[pl.ds(centre, mr)], midx.at[pl.ds(centre - step * mr, mr)]
        )
        start(item)
        pending.append(item)
        near.append(item)
    start(w_up)
    start(w_dn)

    zero_mid = jnp.zeros((mr, lp, mw), F32)
    for at, absent in ((1, first), (0, lat < 2), (3, last), (4, lat >= nl - 2)):
        @pl.when(absent)
        def _():
            midx[pl.ds(at * mr, mr)] = zero_mid

    @pl.when(first)
    def _():
        for row in range(h1):
            fld[row] = jnp.zeros((lp, fw), F32)
            co[row] = jnp.zeros((3, fw), F32)

    @pl.when(last)
    def _():
        for row in range(h1):
            fld[h1 + fr + row] = jnp.zeros((lp, fw), F32)
            co[h1 + fr + row] = jnp.zeros((3, fw), F32)

    for item in (s_up, s_dn, *near, k_up, k_dn):
        wait_recv(item)

    origin = (lat * mr - 2 * mr).astype(F32)

    def weight_of(source, fraction, r):
        place = source - origin
        lower = jnp.where(place == float(r), 1.0 - fraction, 0.0)
        return lower + jnp.where(place == float(r - 1), fraction, 0.0)

    def make_rows(ref, ref_row, ext_row, rows, base):
        def step(i, carry):
            source = jnp.broadcast_to(ref[ref_row + i, 0:1, :], (8, LANES))
            fraction = jnp.broadcast_to(ref[ref_row + i, 1:2, :], (8, LANES))
            weights = [weight_of(source, fraction, base + r) for r in range(3 * mr)]
            for b in range(blocks):
                levels = slice(8 * b, 8 * b + 8)
                pieces = []
                for t in range(qblocks):
                    value = weights[0] * midx[base, levels, t * LANES : (t + 1) * LANES]
                    for r in range(1, 3 * mr):
                        value = value + weights[r] * midx[
                            base + r, levels, t * LANES : (t + 1) * LANES
                        ]
                    pieces.append(value)
                row = jnp.concatenate(pieces, axis=1)
                before = pltpu.roll(row, 1, 1)
                after = pltpu.roll(row, mw - 1, 1)
                at = ext_row + i
                fld[at, levels, 0:mw] = 0.375 * before + 0.625 * row
                fld[at, levels, mw : 2 * mw] = 0.125 * before + 0.875 * row
                fld[at, levels, 2 * mw : 3 * mw] = 0.875 * row + 0.125 * after
                fld[at, levels, 3 * mw : 4 * mw] = 0.625 * row + 0.375 * after
            return carry

        lax.fori_loop(0, rows, step, 0)

    make_rows(sf_ref, 0, h1, fr, mr)

    @pl.when(jnp.logical_not(first))
    def _():
        make_rows(sfr, 0, 0, h1, 0)

    @pl.when(jnp.logical_not(last))
    def _():
        make_rows(sfr, h1, h1 + fr, h1, 2 * mr)

    def one_pass(low, steps):
        for b in range(blocks):
            levels = slice(8 * b, 8 * b + 8)

            def phases(row):
                return [fld[row, levels, p * mw : (p + 1) * mw] for p in range(4)]

            def coef(row, kind, p):
                return co[row, kind : kind + 1, p * mw : (p + 1) * mw]

            centre0 = phases(low)
            under = phases(low - 1)
            flux0 = [coef(low - 1, 0, p) * (centre0[p] - under[p]) for p in range(4)]

            def step(i, carry):
                now, below_flux = carry
                for u in range(UNROLL):
                    row = low + i * UNROLL + u
                    over = phases(row + 1)
                    east = [coef(row, 1, p) * (now[p + 1] - now[p]) for p in range(3)]
                    east.append(coef(row, 1, 3) * (pltpu.roll(now[0], mw - 1, 1) - now[3]))
                    edge = coef(row, 2, 0) * (now[0] - pltpu.roll(now[3], 1, 1))
                    west = [edge] + east[:3]
                    north = [coef(row, 0, p) * (over[p] - now[p]) for p in range(4)]
                    for p in range(4):
                        fld[row, levels, p * mw : (p + 1) * mw] = now[p] + (
                            (north[p] - below_flux[p]) + (east[p] - west[p])
                        )
                    now, below_flux = over, north
                return now, below_flux

            lax.fori_loop(0, steps, step, (centre0, flux0))

    def smooth(margin):
        def body(p, carry):
            low = margin + 1 + p
            one_pass(low, lax.div(ext - 2 * low + UNROLL - 1, UNROLL))

            @pl.when(last)
            def _():
                fld[h1 + fr] = jnp.zeros((lp, fw), F32)

            return carry

        lax.fori_loop(0, PASSES, body, 0)

    smooth(0)
    wait_recv(w_up)
    wait_recv(w_dn)

    def apply_own(i, carry):
        fld[h1 + i] = fld[h1 + i] * wown[i]
        return carry

    lax.fori_loop(0, fr, apply_own, 0)

    @pl.when(jnp.logical_not(first))
    def _():
        for i in range(h2):
            fld[h1 - h2 + i] = fld[h1 - h2 + i] * wrows[0, i]

    @pl.when(jnp.logical_not(last))
    def _():
        for i in range(h2):
            fld[h1 + fr + i] = fld[h1 + fr + i] * wrows[1, i]

    smooth(PASSES)

    def narrow(i, carry):
        for b in range(blocks):
            levels = slice(8 * b, 8 * b + 8)
            g = [fld[h1 + i, levels, p * mw : (p + 1) * mw] for p in range(4)]
            value = 0.625 * (g[0] + g[3]) + 0.875 * (g[1] + g[2])
            value = value + pltpu.roll(0.375 * g[0] + 0.125 * g[1], mw - 1, 1)
            blend[i, levels, :] = value + pltpu.roll(0.125 * g[2] + 0.375 * g[3], 1, 1)
        return carry

    lax.fori_loop(0, fr, narrow, 0)

    def gather(r, carry):
        weights = []
        place_of = (r + mr).astype(F32)
        for f in range(fr):
            source = jnp.broadcast_to(sf_ref[f, 0:1, :], (8, LANES)) - origin
            fraction = jnp.broadcast_to(sf_ref[f, 1:2, :], (8, LANES))
            lower = jnp.where(source == place_of, 1.0 - fraction, 0.0)
            weights.append(lower + jnp.where(source == place_of - 1.0, fraction, 0.0))
        for b in range(blocks):
            levels = slice(8 * b, 8 * b + 8)
            for t in range(qblocks):
                lanes = slice(t * LANES, (t + 1) * LANES)
                value = weights[0] * blend[0, levels, lanes]
                for f in range(1, fr):
                    value = value + weights[f] * blend[f, levels, lanes]
                contrib[r, levels, lanes] = value
        return carry

    lax.fori_loop(0, 3 * mr, gather, 0)
    a_up = lat_copy(12, 1, contrib.at[pl.ds(2 * mr, mr)], adjr.at[0])
    a_dn = lat_copy(13, -1, contrib.at[pl.ds(0, mr)], adjr.at[1])
    for item in (a_up, a_dn):
        start(item)
        pending.append(item)
    for at, absent in ((0, first), (1, last)):
        @pl.when(absent)
        def _():
            adjr[at] = zero_mid
    wait_recv(a_up)
    wait_recv(a_dn)
    fa[:, mine, :] = contrib[pl.ds(mr, mr)] + (adjr[0] + adjr[1])

    ag = []
    for k in range(1, nm):
        target = lax.rem(mem + k, nm)
        copy = pltpu.make_async_remote_copy(
            src_ref=fa.at[:, mine, :], dst_ref=fa.at[:, mine, :],
            send_sem=send_sem.at[16 + nm + k], recv_sem=recv_sem.at[16 + nm + k],
            device_id={"mem": target}, device_id_type=MESH,
        )
        copy.start()
        ag.append(copy)
    for k in range(1, nm):
        ag[k - 1].wait_recv()
    for copy in rs:
        copy.wait_send()
    for r in range(mr):
        for t in range(qblocks):
            ls[t, pl.ds(r, lv, stride=mr), :] = fa[r, :, t * LANES : (t + 1) * LANES]
    spread = jnp.concatenate([ls[t] for t in range(qblocks)], axis=1)

    down = down_ref[...]
    lont = lont_ref[...]
    for m in range(mb):
        parts = split3(pert[m].astype(F32) * spread)
        tall = dot(down, parts[0]) + (dot(down, parts[1]) + dot(down, parts[2]))
        thin = split3(tall)
        grad = dot(thin[0], lont) + (dot(thin[1], lont) + dot(thin[2], lont))
        for c in range(3):
            gp[c, m] = grad[c * cl : (c + 1) * cl]
    g_up = lat_copy(14, 1, gp.at[2], gpr.at[0])
    g_dn = lat_copy(15, -1, gp.at[0], gpr.at[1])
    for item in (g_up, g_dn):
        start(item)
        pending.append(item)

    @pl.when(first)
    def _():
        gpr[0] = gp[0]

    @pl.when(last)
    def _():
        gpr[1] = gp[2]

    wait_recv(g_up)
    wait_recv(g_dn)
    out_ref[...] = ctl_ref[...] + (gp[1] + (gpr[0] + gpr[1]))
    for item in pending:
        wait_send(item)
    for copy in ag:
        copy.wait_send()


def body(controls, perturbations, precision_weight, north_coef, east_coef, fine_source, fine_frac):
    nm, nl = lax.axis_size("mem"), lax.axis_size("lat")
    mb, cl, _, cw = controls.shape
    _, lv, mr, mw = perturbations.shape
    fr, fw = north_coef.shape
    lp = lv // nm
    h1, h2 = 2 * PASSES, PASSES
    ext = fr + 2 * h1
    level = refine_matrix(cl, "edge")
    across = refine_matrix(1, "pad")
    up = np.einsum("vc,ra->vrac", level, across).reshape(lv * mr, 3 * cl)
    lon = refine_matrix(cw, "wrap").T
    sf = jnp.stack([fine_source.astype(F32), fine_frac], axis=1)
    sf = jnp.broadcast_to(sf[:, :, None], (fr, 2, LANES))
    vmem = pl.BlockSpec(memory_space=pltpu.VMEM)
    anywhere = pl.BlockSpec(memory_space=pl.ANY)
    dims = (nm, nl, mb, cl, cw, lv, mr, mw, fr, fw)
    slots = 17 + 2 * nm
    result = pl.pallas_call(
        functools.partial(kernel, dims),
        out_shape=jax.ShapeDtypeStruct((mb, cl, cw), F32),
        in_specs=[vmem, anywhere, anywhere] + [vmem] * 7,
        out_specs=vmem,
        scratch_shapes=[
            pltpu.VMEM((2, mb, cl, cw), F32),
            pltpu.VMEM((mb, lv * mr, mw), BF16),
            pltpu.VMEM((lp, fr, fw), BF16),
            pltpu.VMEM((2, h2, lp, fw), F32),
            pltpu.VMEM((ext + UNROLL, 3, fw), F32),
            pltpu.VMEM((2 * h1, 2, LANES), F32),
            pltpu.VMEM((mw // LANES, lv * mr, LANES), F32),
            pltpu.VMEM((mr, lv, mw), F32),
            pltpu.VMEM((nm - 1, mr, lp, mw), F32),
            pltpu.VMEM((5 * mr, lp, mw), F32),
            pltpu.VMEM((ext + UNROLL, lp, fw), F32),
            pltpu.VMEM((fr, lp, mw), F32),
            pltpu.VMEM((3 * mr, lp, mw), F32),
            pltpu.VMEM((2, mr, lp, mw), F32),
            pltpu.VMEM((mr, lv, mw), F32),
            pltpu.VMEM((3, mb, cl, cw), F32),
            pltpu.VMEM((2, mb, cl, cw), F32),
            pltpu.VMEM((fr, lp, fw), F32),
            pltpu.SemaphoreType.DMA((2,)),
            pltpu.SemaphoreType.DMA((slots,)),
            pltpu.SemaphoreType.DMA((slots,)),
        ],
        compiler_params=pltpu.CompilerParams(collective_id=0, has_side_effects=True),
    )(
        controls.reshape(mb, cl, cw),
        perturbations.reshape(mb, lv * mr, mw),
        precision_weight,
        north_coef,
        east_coef,
        sf,
        jnp.asarray(np.concatenate([up] * 3, axis=1), BF16),
        jnp.asarray(lon, BF16),
        jnp.asarray(up.T, BF16),
        jnp.asarray(lon.T, BF16),
    )
    return result.reshape(controls.shape)


def solution(mesh):
    in_specs = (
        P("mem", None, "lat", None),
        P("mem", None, "lat", None),
        P(None, "lat", None),
        P("lat", None),
        P("lat", None),
        P("lat"),
        P("lat"),
    )
    out_specs = P("mem", None, "lat", None)
    return jax.shard_map(body, mesh=mesh, in_specs=in_specs, out_specs=out_specs, check_vma=False)
```

```python
import functools
import jax
import jax.numpy as jnp
import numpy as np
from jax import lax
from jax.experimental import pallas as pl
from jax.experimental.pallas import tpu as pltpu
from jax.sharding import PartitionSpec as P

PASSES = 5
REACH = 4
LANES = 128
UNROLL = 8
F32 = jnp.float32
BF16 = jnp.bfloat16
MESH = pl.DeviceIdType.MESH


def refine_matrix(count, mode):
    weights = [(0.375, 0.625, 0.0), (0.125, 0.875, 0.0), (0.0, 0.875, 0.125), (0.0, 0.625, 0.375)]
    full = np.zeros((4 * count, count + 2), np.float32)
    for q in range(count):
        for r in range(4):
            full[4 * q + r, q : q + 3] += weights[r]
    if mode == "pad":
        return full
    inner = full[:, 1:-1].copy()
    if mode == "edge":
        inner[:, 0] += full[:, 0]
        inner[:, -1] += full[:, -1]
    else:
        inner[:, -1] += full[:, 0]
        inner[:, 0] += full[:, -1]
    return inner


def split3(value):
    high = value.astype(BF16)
    rest = value - high.astype(F32)
    mid = rest.astype(BF16)
    low = (rest - mid.astype(F32)).astype(BF16)
    return high, mid, low


def dot(a, b):
    return jnp.dot(a, b, preferred_element_type=F32)


def kernel(
    dims,
    ctl_ref, pert_hbm, pw_hbm, north_ref, east_ref, source_ref, frac_ref, up_ref, lon_ref, down_ref, lont_ref,
    out_ref,
    ctl, pert, pw, wrows, co, wt, ls, mids, rsr, midx, fld, blend, contrib, adjr, fa, gp, gpr, wown,
    local_sem, send_sem, recv_sem,
):
    nm, nl, mb, cl, cw, lv, mr, mw, fr, fw = dims
    lp = lv // nm
    h1, h2 = 2 * PASSES, PASSES
    ext = fr + 2 * h1
    mem, lat = lax.axis_index("mem"), lax.axis_index("lat")
    first, last = lat == 0, lat == nl - 1
    blocks = lp // 8
    taps = wt.shape[1]

    cp_pert = pltpu.make_async_copy(pert_hbm, pert, local_sem.at[0])
    cp_pert.start()
    cp_pw = pltpu.make_async_copy(
        pw_hbm.at[pl.ds(mem * lp, lp)], pw, local_sem.at[1]
    )
    cp_pw.start()

    barrier = pltpu.get_barrier_semaphore()
    for step in (1, 2):
        @pl.when(lat >= step)
        def _():
            pl.semaphore_signal(barrier, inc=1, device_id={"lat": lat - step}, device_id_type=MESH)

        @pl.when(lat < nl - step)
        def _():
            pl.semaphore_signal(barrier, inc=1, device_id={"lat": lat + step}, device_id_type=MESH)
    for k in range(1, nm):
        pl.semaphore_signal(
            barrier, inc=1, device_id={"mem": lax.rem(mem + k, nm)}, device_id_type=MESH
        )
    present = nm - 1
    for step in (1, 2):
        present = present + (lat >= step).astype(jnp.int32) + (lat < nl - step).astype(jnp.int32)

    spot = lax.broadcasted_iota(jnp.int32, (taps, LANES), 0)
    for row in range(fr):
        place = source_ref[row] - (lat * mr - mr)
        upper = jnp.full((taps, LANES), frac_ref[row], F32)
        wt[h1 + row] = jnp.where(
            spot == place, 1.0 - upper, jnp.where(spot == place + 1, upper, 0.0)
        )

    rows_i = lax.broadcasted_iota(jnp.int32, (4 * LANES, 4 * LANES), 0)
    cols_i = lax.broadcasted_iota(jnp.int32, (4 * LANES, 4 * LANES), 1)
    perm = (rows_i == 4 * lax.rem(cols_i, LANES) + lax.div(cols_i, LANES)).astype(F32).astype(BF16)
    qblocks = mw // LANES

    for kind, ref in enumerate((north_ref, east_ref)):
        stacked = jnp.concatenate(split3(ref[...]), axis=0)
        edges = []
        for block in range(qblocks):
            moved = dot(stacked[:, block * 4 * LANES : (block + 1) * 4 * LANES], perm)
            exact = (moved[:fr] + moved[fr : 2 * fr]) + moved[2 * fr :]
            edges.append(exact[:, 3 * LANES :])
            for phase in range(4):
                lanes = pl.ds(phase * mw + block * LANES, LANES)
                for row in range(fr):
                    co[h1 + row, kind : kind + 1, lanes] = exact[
                        row : row + 1, phase * LANES : (phase + 1) * LANES
                    ]
    edge = pltpu.roll(jnp.concatenate(edges, axis=1), 1, 1)
    for row in range(fr):
        co[h1 + row, 2:3, 0:mw] = edge[row : row + 1]
        co[h1 + row, 2:3, mw:fw] = jnp.zeros((1, fw - mw), F32)
    pl.semaphore_wait(barrier, present)

    def lat_copy(slot, step, src, dst):
        copy = pltpu.make_async_remote_copy(
            src_ref=src, dst_ref=dst, send_sem=send_sem.at[slot], recv_sem=recv_sem.at[slot],
            device_id={"lat": lat + step}, device_id_type=MESH,
        )
        if step > 0:
            return copy, lat < nl - step, lat >= step
        return copy, lat >= -step, lat < nl + step

    def start(item):
        copy, sends, _ = item

        @pl.when(sends)
        def _():
            copy.start()

    def wait_recv(item):
        copy, _, receives = item

        @pl.when(receives)
        def _():
            copy.wait_recv()

    def wait_send(item):
        copy, sends, _ = item

        @pl.when(sends)
        def _():
            copy.wait_send()

    pending = []

    c_up = lat_copy(0, 1, ctl_ref, ctl.at[0])
    c_dn = lat_copy(1, -1, ctl_ref, ctl.at[1])
    k_up = lat_copy(4, 1, co.at[pl.ds(fr, h1)], co.at[pl.ds(0, h1)])
    k_dn = lat_copy(5, -1, co.at[pl.ds(h1, h1)], co.at[pl.ds(h1 + fr, h1)])
    s_up = lat_copy(2, 1, wt.at[pl.ds(fr, h1)], wt.at[pl.ds(0, h1)])
    s_dn = lat_copy(3, -1, wt.at[pl.ds(h1, h1)], wt.at[pl.ds(h1 + fr, h1)])
    for item in (c_up, c_dn, s_up, s_dn, k_up, k_dn):
        start(item)
        pending.append(item)

    cp_pw.wait()
    count = lp * fr
    to_i = lax.broadcasted_iota(jnp.int32, (count, count), 0)
    from_i = lax.broadcasted_iota(jnp.int32, (count, count), 1)
    turn = (from_i == lax.rem(to_i, lp) * fr + lax.div(to_i, lp)).astype(F32).astype(BF16)
    for block in range(qblocks):
        piece = pw[:, :, block * 4 * LANES : (block + 1) * 4 * LANES].reshape(count, 4 * LANES)
        turned = dot(turn, piece).astype(BF16)
        moved = dot(turned, perm)
        for phase in range(4):
            lanes = pl.ds(phase * mw + block * LANES, LANES)
            wown[:, :, lanes] = moved[:, phase * LANES : (phase + 1) * LANES].reshape(fr, lp, LANES)
    w_up = lat_copy(6, 1, wown.at[pl.ds(fr - h2, h2)], wrows.at[0])
    w_dn = lat_copy(7, -1, wown.at[pl.ds(0, h2)], wrows.at[1])
    for item in (w_up, w_dn):
        start(item)
        pending.append(item)

    wait_recv(c_up)
    wait_recv(c_dn)
    own = ctl_ref[...]
    below = jnp.where(first, own, ctl[0])
    above = jnp.where(last, own, ctl[1])
    lon = lon_ref[...]
    wide = []
    for part in (below, own, above):
        parts = split3(part.reshape(mb * cl, cw))
        wide.append(dot(parts[0], lon) + (dot(parts[1], lon) + dot(parts[2], lon)))
    cp_pert.wait()
    up3 = up_ref[...]
    for m in range(mb):
        stack = jnp.concatenate([w[m * cl : (m + 1) * cl] for w in wide], axis=0)
        raised = dot(up3, jnp.concatenate(split3(stack), axis=0))
        term = pert[m].astype(F32).reshape(lv * mr, mw) * raised
        for t in range(qblocks):
            piece = term[:, t * LANES : (t + 1) * LANES]
            if m == 0:
                ls[t] = piece
            else:
                ls[t] += piece
    for r in range(mr):
        for t in range(qblocks):
            mids[r, :, t * LANES : (t + 1) * LANES] = ls[t, pl.ds(r, lv, stride=mr), :]

    def block_levels(b):
        return pl.ds(8 * b, 8)

    def mem_slice(device, b):
        return pl.ds(pl.multiple_of(device * lp + 8 * b, 8), 8)

    rs = {}
    for b in range(blocks):
        for k in range(1, nm):
            target = lax.rem(mem + k, nm)
            slot = 10 + 6 * blocks + (b * nm + k)
            copy = pltpu.make_async_remote_copy(
                src_ref=mids.at[:, mem_slice(target, b), :],
                dst_ref=rsr.at[k - 1, :, block_levels(b), :],
                send_sem=send_sem.at[slot], recv_sem=recv_sem.at[slot],
                device_id={"mem": target}, device_id_type=MESH,
            )
            copy.start()
            rs[b, k] = copy

    centre = 2 * mr
    zero_mid = jnp.zeros((mr, lp, mw), F32)
    for at, absent in ((1, first), (0, lat < 2), (3, last), (4, lat >= nl - 2)):
        @pl.when(absent)
        def _():
            midx[pl.ds(at * mr, mr)] = zero_mid

    @pl.when(first)
    def _():
        adjr[0] = zero_mid
        for row in range(h1):
            fld[row] = jnp.zeros((lp, fw), F32)
            co[row] = jnp.zeros((3, fw), F32)

    @pl.when(last)
    def _():
        adjr[1] = zero_mid
        for row in range(h1):
            fld[h1 + fr + row] = jnp.zeros((lp, fw), F32)
            co[h1 + fr + row] = jnp.zeros((3, fw), F32)

    def add_up(b):
        levels = slice(8 * b, 8 * b + 8)
        total = mids[:, mem_slice(mem, b), :]
        for k in range(1, nm):
            rs[b, k].wait_recv()
            total = total + rsr[k - 1, :, levels, :]
        midx[pl.ds(centre, mr), levels, :] = total
        items = []
        for place, step in enumerate((1, -1, 2, -2)):
            item = lat_copy(
                10 + 4 * b + place, step,
                midx.at[pl.ds(centre, mr), block_levels(b), :],
                midx.at[pl.ds(centre - step * mr, mr), block_levels(b), :],
            )
            start(item)
            pending.append(item)
            items.append(item)
        return items

    def make_rows(b, at, rows, base, unroll):
        levels = slice(8 * b, 8 * b + 8)

        def one(i):
            row = []
            shares = [
                jnp.broadcast_to(wt[i, r : r + 1, :], (8, LANES)) for r in range(3 * mr)
            ]
            for t in range(qblocks):
                lanes = slice(t * LANES, (t + 1) * LANES)
                value = shares[0] * midx[base, levels, lanes]
                for r in range(1, 3 * mr):
                    value = value + shares[r] * midx[base + r, levels, lanes]
                row.append(value)
            row = jnp.concatenate(row, axis=1)
            before = pltpu.roll(row, 1, 1)
            after = pltpu.roll(row, mw - 1, 1)
            fld[i, levels, 0:mw] = 0.375 * before + 0.625 * row
            fld[i, levels, mw : 2 * mw] = 0.125 * before + 0.875 * row
            fld[i, levels, 2 * mw : 3 * mw] = 0.875 * row + 0.125 * after
            fld[i, levels, 3 * mw : 4 * mw] = 0.625 * row + 0.375 * after

        def step(i, carry):
            for u in range(unroll):
                one(at + i * unroll + u)
            return carry

        lax.fori_loop(0, rows // unroll, step, 0)

    def one_pass(b, low, steps):
        levels = slice(8 * b, 8 * b + 8)

        def phases(row):
            return [fld[row, levels, p * mw : (p + 1) * mw] for p in range(4)]

        def coef(row, kind, p):
            return co[row, kind : kind + 1, p * mw : (p + 1) * mw]

        centre0 = phases(low)
        under = phases(low - 1)
        flux0 = [coef(low - 1, 0, p) * (centre0[p] - under[p]) for p in range(4)]

        def step(i, carry):
            now, below_flux = carry
            for u in range(UNROLL):
                row = low + i * UNROLL + u
                over = phases(row + 1)
                east = [coef(row, 1, p) * (now[p + 1] - now[p]) for p in range(3)]
                east.append(coef(row, 1, 3) * (pltpu.roll(now[0], mw - 1, 1) - now[3]))
                edge = coef(row, 2, 0) * (now[0] - pltpu.roll(now[3], 1, 1))
                west = [edge] + east[:3]
                north = [coef(row, 0, p) * (over[p] - now[p]) for p in range(4)]
                for p in range(4):
                    fld[row, levels, p * mw : (p + 1) * mw] = now[p] + (
                        (north[p] - below_flux[p]) + (east[p] - west[p])
                    )
                now, below_flux = over, north
            return now, below_flux

        lax.fori_loop(0, steps, step, (centre0, flux0))

    def smooth(b, margin):
        levels = slice(8 * b, 8 * b + 8)

        def body(p, carry):
            low = margin + 1 + p
            one_pass(b, low, lax.div(ext - 2 * low + UNROLL - 1, UNROLL))

            @pl.when(last)
            def _():
                fld[h1 + fr, levels, :] = jnp.zeros((8, fw), F32)

            return carry

        lax.fori_loop(0, PASSES, body, 0)

    def apply_weights(b):
        levels = slice(8 * b, 8 * b + 8)

        def apply_own(i, carry):
            for u in range(4):
                row = 4 * i + u
                fld[h1 + row, levels, :] = fld[h1 + row, levels, :] * wown[row, levels, :]
            return carry

        lax.fori_loop(0, fr // 4, apply_own, 0)

        @pl.when(jnp.logical_not(first))
        def _():
            for i in range(h2):
                at = h1 - h2 + i
                fld[at, levels, :] = fld[at, levels, :] * wrows[0, i, levels, :]

        @pl.when(jnp.logical_not(last))
        def _():
            for i in range(h2):
                at = h1 + fr + i
                fld[at, levels, :] = fld[at, levels, :] * wrows[1, i, levels, :]

    def transpose_rows(b):
        levels = slice(8 * b, 8 * b + 8)

        def narrow(step, carry):
            for u in range(4):
                i = 4 * step + u
                g = [fld[h1 + i, levels, p * mw : (p + 1) * mw] for p in range(4)]
                value = 0.625 * (g[0] + g[3]) + 0.875 * (g[1] + g[2])
                value = value + pltpu.roll(0.375 * g[0] + 0.125 * g[1], mw - 1, 1)
                blend[i, levels, :] = value + pltpu.roll(0.125 * g[2] + 0.375 * g[3], 1, 1)
            return carry

        lax.fori_loop(0, fr // 4, narrow, 0)

        def gather(r):
            shares = [
                jnp.broadcast_to(wt[h1 + f, r : r + 1, :], (8, LANES)) for f in range(fr)
            ]
            for t in range(qblocks):
                lanes = slice(t * LANES, (t + 1) * LANES)
                value = shares[0] * blend[0, levels, lanes]
                for f in range(1, fr):
                    value = value + shares[f] * blend[f, levels, lanes]
                contrib[r, levels, lanes] = value

        for r in list(range(mr)) + list(range(2 * mr, 3 * mr)):
            gather(r)
        items = []
        for place, step, at in ((0, 1, 2 * mr), (1, -1, 0)):
            item = lat_copy(
                10 + 4 * blocks + 2 * b + place, step,
                contrib.at[pl.ds(at, mr), block_levels(b), :],
                adjr.at[place, :, block_levels(b), :],
            )
            start(item)
            pending.append(item)
            items.append(item)
        for r in range(mr, 2 * mr):
            gather(r)
        return items

    ag = {}

    def share(b, items):
        levels = slice(8 * b, 8 * b + 8)
        for item in items:
            wait_recv(item)
        mine = mem_slice(mem, b)
        fa[:, mine, :] = contrib[pl.ds(mr, mr), levels, :] + (
            adjr[0, :, levels, :] + adjr[1, :, levels, :]
        )
        for k in range(1, nm):
            target = lax.rem(mem + k, nm)
            slot = 10 + 6 * blocks + ((blocks + b) * nm + k)
            copy = pltpu.make_async_remote_copy(
                src_ref=fa.at[:, mine, :], dst_ref=fa.at[:, mine, :],
                send_sem=send_sem.at[slot], recv_sem=recv_sem.at[slot],
                device_id={"mem": target}, device_id_type=MESH,
            )
            copy.start()
            ag[b, k] = copy

    near = {0: add_up(0)}
    previous = None
    for b in range(blocks):
        if b == 0:
            wait_recv(s_up)
            wait_recv(s_dn)
        for item in near[b][:2]:
            wait_recv(item)
        make_rows(b, h1, fr, mr, 4)
        for item in near[b][2:]:
            wait_recv(item)

        @pl.when(jnp.logical_not(first))
        def _():
            make_rows(b, 0, h1, 0, 5)

        @pl.when(jnp.logical_not(last))
        def _():
            make_rows(b, h1 + fr, h1, 2 * mr, 5)

        if b + 1 < blocks:
            near[b + 1] = add_up(b + 1)
        if b == 0:
            wait_recv(k_up)
            wait_recv(k_dn)
        smooth(b, 0)
        if previous is not None:
            share(b - 1, previous)
        if b == 0:
            wait_recv(w_up)
            wait_recv(w_dn)
        apply_weights(b)
        smooth(b, PASSES)
        previous = transpose_rows(b)
    share(blocks - 1, previous)
    for copy in ag.values():
        copy.wait_recv()
    for copy in rs.values():
        copy.wait_send()
    for r in range(mr):
        for t in range(qblocks):
            ls[t, pl.ds(r, lv, stride=mr), :] = fa[r, :, t * LANES : (t + 1) * LANES]
    spread = jnp.concatenate([ls[t] for t in range(qblocks)], axis=1)

    down = down_ref[...]
    lont = lont_ref[...]
    for m in range(mb):
        parts = split3(pert[m].astype(F32).reshape(lv * mr, mw) * spread)
        tall = dot(down, parts[0]) + (dot(down, parts[1]) + dot(down, parts[2]))
        thin = split3(tall)
        grad = dot(thin[0], lont) + (dot(thin[1], lont) + dot(thin[2], lont))
        for c in range(3):
            gp[c, m] = grad[c * cl : (c + 1) * cl]
    g_up = lat_copy(8, 1, gp.at[2], gpr.at[0])
    g_dn = lat_copy(9, -1, gp.at[0], gpr.at[1])
    for item in (g_up, g_dn):
        start(item)
        pending.append(item)

    @pl.when(first)
    def _():
        gpr[0] = gp[0]

    @pl.when(last)
    def _():
        gpr[1] = gp[2]

    wait_recv(g_up)
    wait_recv(g_dn)
    out_ref[...] = ctl_ref[...] + (gp[1] + (gpr[0] + gpr[1]))
    for item in pending:
        wait_send(item)
    for copy in ag.values():
        copy.wait_send()


def body(controls, perturbations, precision_weight, north_coef, east_coef, fine_source, fine_frac):
    nm, nl = lax.axis_size("mem"), lax.axis_size("lat")
    mb, cl, _, cw = controls.shape
    _, lv, mr, mw = perturbations.shape
    fr, fw = north_coef.shape
    lp = lv // nm
    h1, h2 = 2 * PASSES, PASSES
    ext = fr + 2 * h1
    level = refine_matrix(cl, "edge")
    across = refine_matrix(1, "pad")
    up = np.einsum("vc,ra->vrac", level, across).reshape(lv * mr, 3 * cl)
    lon = refine_matrix(cw, "wrap").T
    vmem = pl.BlockSpec(memory_space=pltpu.VMEM)
    smem = pl.BlockSpec(memory_space=pltpu.SMEM)
    anywhere = pl.BlockSpec(memory_space=pl.ANY)
    dims = (nm, nl, mb, cl, cw, lv, mr, mw, fr, fw)
    blocks = lp // 8
    slots = 10 + 6 * blocks + 2 * blocks * nm
    taps = -(-3 * mr // 8) * 8
    result = pl.pallas_call(
        functools.partial(kernel, dims),
        out_shape=jax.ShapeDtypeStruct((mb, cl, cw), F32),
        in_specs=[vmem, anywhere, anywhere, vmem, vmem, smem, smem] + [vmem] * 4,
        out_specs=vmem,
        scratch_shapes=[
            pltpu.VMEM((2, mb, cl, cw), F32),
            pltpu.VMEM((mb, lv, mr, mw), BF16),
            pltpu.VMEM((lp, fr, fw), BF16),
            pltpu.VMEM((2, h2, lp, fw), F32),
            pltpu.VMEM((ext + UNROLL, 3, fw), F32),
            pltpu.VMEM((ext, taps, LANES), F32),
            pltpu.VMEM((mw // LANES, lv * mr, LANES), F32),
            pltpu.VMEM((mr, lv, mw), F32),
            pltpu.VMEM((nm - 1, mr, lp, mw), F32),
            pltpu.VMEM((5 * mr, lp, mw), F32),
            pltpu.VMEM((ext + UNROLL, lp, fw), F32),
            pltpu.VMEM((fr, lp, mw), F32),
            pltpu.VMEM((3 * mr, lp, mw), F32),
            pltpu.VMEM((2, mr, lp, mw), F32),
            pltpu.VMEM((mr, lv, mw), F32),
            pltpu.VMEM((3, mb, cl, cw), F32),
            pltpu.VMEM((2, mb, cl, cw), F32),
            pltpu.VMEM((fr, lp, fw), F32),
            pltpu.SemaphoreType.DMA((2,)),
            pltpu.SemaphoreType.DMA((slots,)),
            pltpu.SemaphoreType.DMA((slots,)),
        ],
        compiler_params=pltpu.CompilerParams(collective_id=0, has_side_effects=True),
    )(
        controls.reshape(mb, cl, cw),
        perturbations,
        precision_weight,
        north_coef,
        east_coef,
        fine_source,
        fine_frac,
        jnp.asarray(np.concatenate([up] * 3, axis=1), BF16),
        jnp.asarray(lon, BF16),
        jnp.asarray(up.T, BF16),
        jnp.asarray(lon.T, BF16),
    )
    return result.reshape(controls.shape)


def solution(mesh):
    in_specs = (
        P("mem", None, "lat", None),
        P("mem", None, "lat", None),
        P(None, "lat", None),
        P("lat", None),
        P("lat", None),
        P("lat"),
        P("lat"),
    )
    out_specs = P("mem", None, "lat", None)
    return jax.shard_map(body, mesh=mesh, in_specs=in_specs, out_specs=out_specs, check_vma=False)
```

```python
import functools
import jax
import jax.numpy as jnp
import numpy as np
from jax import lax
from jax.experimental import pallas as pl
from jax.experimental.pallas import tpu as pltpu
from jax.sharding import PartitionSpec as P

PASSES = 5
REACH = 4
LANES = 128
UNROLL = 8
F32 = jnp.float32
BF16 = jnp.bfloat16
MESH = pl.DeviceIdType.MESH


def refine_matrix(count, mode):
    weights = [(0.375, 0.625, 0.0), (0.125, 0.875, 0.0), (0.0, 0.875, 0.125), (0.0, 0.625, 0.375)]
    full = np.zeros((4 * count, count + 2), np.float32)
    for q in range(count):
        for r in range(4):
            full[4 * q + r, q : q + 3] += weights[r]
    if mode == "pad":
        return full
    inner = full[:, 1:-1].copy()
    if mode == "edge":
        inner[:, 0] += full[:, 0]
        inner[:, -1] += full[:, -1]
    else:
        inner[:, -1] += full[:, 0]
        inner[:, 0] += full[:, -1]
    return inner


def split3(value):
    high = value.astype(BF16)
    rest = value - high.astype(F32)
    mid = rest.astype(BF16)
    low = (rest - mid.astype(F32)).astype(BF16)
    return high, mid, low


def split2(value):
    high = value.astype(BF16)
    return high, (value - high.astype(F32)).astype(BF16)


def dot(a, b):
    return jnp.dot(a, b, preferred_element_type=F32)


def kernel(
    dims,
    ctl_ref, pert_hbm, pw_hbm, north_ref, east_ref, source_ref, frac_ref, up_ref, lon_ref, down_ref, lont_ref,
    out_ref,
    ctl, pert, pw, wrows, co, wt, ls, mids, rsr, midx, fld, blend, contrib, adjr, fa, gp, gpr, wown, tall,
    local_sem, send_sem, recv_sem,
):
    nm, nl, mb, cl, cw, lv, mr, mw, fr, fw = dims
    lp = lv // nm
    h1, h2 = 2 * PASSES, PASSES
    ext = fr + 2 * h1
    mem, lat = lax.axis_index("mem"), lax.axis_index("lat")
    first, last = lat == 0, lat == nl - 1
    blocks = lp // 8
    taps = wt.shape[1]

    cp_pert = pltpu.make_async_copy(pert_hbm, pert, local_sem.at[0])
    cp_pert.start()
    cp_pw = pltpu.make_async_copy(
        pw_hbm.at[pl.ds(mem * lp, lp)], pw, local_sem.at[1]
    )
    cp_pw.start()

    barrier = pltpu.get_barrier_semaphore()
    for step in (1, 2):
        @pl.when(lat >= step)
        def _():
            pl.semaphore_signal(barrier, inc=1, device_id={"lat": lat - step}, device_id_type=MESH)

        @pl.when(lat < nl - step)
        def _():
            pl.semaphore_signal(barrier, inc=1, device_id={"lat": lat + step}, device_id_type=MESH)
    for k in range(1, nm):
        pl.semaphore_signal(
            barrier, inc=1, device_id={"mem": lax.rem(mem + k, nm)}, device_id_type=MESH
        )
    present = nm - 1
    for step in (1, 2):
        present = present + (lat >= step).astype(jnp.int32) + (lat < nl - step).astype(jnp.int32)

    spot = lax.broadcasted_iota(jnp.int32, (taps, LANES), 0)
    for row in range(fr):
        place = source_ref[row] - (lat * mr - mr)
        upper = jnp.full((taps, LANES), frac_ref[row], F32)
        wt[h1 + row] = jnp.where(
            spot == place, 1.0 - upper, jnp.where(spot == place + 1, upper, 0.0)
        )

    rows_i = lax.broadcasted_iota(jnp.int32, (4 * LANES, 4 * LANES), 0)
    cols_i = lax.broadcasted_iota(jnp.int32, (4 * LANES, 4 * LANES), 1)
    perm = (rows_i == 4 * lax.rem(cols_i, LANES) + lax.div(cols_i, LANES)).astype(F32).astype(BF16)
    qblocks = mw // LANES

    for kind, ref in enumerate((north_ref, east_ref)):
        stacked = jnp.concatenate(split3(ref[...]), axis=0)
        edges = []
        for block in range(qblocks):
            moved = dot(stacked[:, block * 4 * LANES : (block + 1) * 4 * LANES], perm)
            exact = (moved[:fr] + moved[fr : 2 * fr]) + moved[2 * fr :]
            edges.append(exact[:, 3 * LANES :])
            for phase in range(4):
                lanes = pl.ds(phase * mw + block * LANES, LANES)
                for row in range(fr):
                    co[h1 + row, kind : kind + 1, lanes] = exact[
                        row : row + 1, phase * LANES : (phase + 1) * LANES
                    ]
    edge = pltpu.roll(jnp.concatenate(edges, axis=1), 1, 1)
    for row in range(fr):
        co[h1 + row, 2:3, 0:mw] = edge[row : row + 1]
        co[h1 + row, 2:3, mw:fw] = jnp.zeros((1, fw - mw), F32)
    pl.semaphore_wait(barrier, present)

    def lat_copy(slot, step, src, dst):
        copy = pltpu.make_async_remote_copy(
            src_ref=src, dst_ref=dst, send_sem=send_sem.at[slot], recv_sem=recv_sem.at[slot],
            device_id={"lat": lat + step}, device_id_type=MESH,
        )
        if step > 0:
            return copy, lat < nl - step, lat >= step
        return copy, lat >= -step, lat < nl + step

    def start(item):
        copy, sends, _ = item

        @pl.when(sends)
        def _():
            copy.start()

    def wait_recv(item):
        copy, _, receives = item

        @pl.when(receives)
        def _():
            copy.wait_recv()

    def wait_send(item):
        copy, sends, _ = item

        @pl.when(sends)
        def _():
            copy.wait_send()

    pending = []

    c_up = lat_copy(0, 1, ctl_ref, ctl.at[0])
    c_dn = lat_copy(1, -1, ctl_ref, ctl.at[1])
    k_up = lat_copy(4, 1, co.at[pl.ds(fr, h1)], co.at[pl.ds(0, h1)])
    k_dn = lat_copy(5, -1, co.at[pl.ds(h1, h1)], co.at[pl.ds(h1 + fr, h1)])
    s_up = lat_copy(2, 1, wt.at[pl.ds(fr, h1)], wt.at[pl.ds(0, h1)])
    s_dn = lat_copy(3, -1, wt.at[pl.ds(h1, h1)], wt.at[pl.ds(h1 + fr, h1)])
    for item in (c_up, c_dn, s_up, s_dn, k_up, k_dn):
        start(item)
        pending.append(item)

    cp_pw.wait()
    count = lp * fr
    to_i = lax.broadcasted_iota(jnp.int32, (count, count), 0)
    from_i = lax.broadcasted_iota(jnp.int32, (count, count), 1)
    turn = (from_i == lax.rem(to_i, lp) * fr + lax.div(to_i, lp)).astype(F32).astype(BF16)
    for block in range(qblocks):
        piece = pw[:, :, block * 4 * LANES : (block + 1) * 4 * LANES].reshape(count, 4 * LANES)
        turned = dot(turn, piece).astype(BF16)
        moved = dot(turned, perm)
        for phase in range(4):
            lanes = pl.ds(phase * mw + block * LANES, LANES)
            wown[:, :, lanes] = moved[:, phase * LANES : (phase + 1) * LANES].reshape(fr, lp, LANES)
    w_up = lat_copy(6, 1, wown.at[pl.ds(fr - h2, h2)], wrows.at[0])
    w_dn = lat_copy(7, -1, wown.at[pl.ds(0, h2)], wrows.at[1])
    pending += [w_up, w_dn]

    wait_recv(c_up)
    wait_recv(c_dn)
    own = ctl_ref[...]
    below = jnp.where(first, own, ctl[0])
    above = jnp.where(last, own, ctl[1])
    lon = lon_ref[...]
    wide = []
    for part in (below, own, above):
        parts = split2(part.reshape(mb * cl, cw))
        wide.append(dot(parts[0], lon) + dot(parts[1], lon))
    cp_pert.wait()
    def block_levels(b):
        return pl.ds(8 * b, 8)

    def mem_slice(device, b):
        return pl.ds(pl.multiple_of(device * lp + 8 * b, 8), 8)

    stacks = []
    for m in range(mb):
        stack = jnp.concatenate([w[m * cl : (m + 1) * cl] for w in wide], axis=0)
        stacks.append(jnp.concatenate(split2(stack), axis=0))
    part = lp * mr
    rs = {}

    def send_sum(b, k):
        target = lax.rem(mem + k, nm)
        slot = 10 + 6 * blocks + (b * nm + k)
        copy = pltpu.make_async_remote_copy(
            src_ref=mids.at[:, mem_slice(target, b), :],
            dst_ref=rsr.at[k - 1, :, block_levels(b), :],
            send_sem=send_sem.at[slot], recv_sem=recv_sem.at[slot],
            device_id={"mem": target}, device_id_type=MESH,
        )
        copy.start()
        rs[b, k] = copy

    for k in list(range(1, nm)) + [0]:
        target = lax.rem(mem + k, nm)
        up2 = up_ref[pl.ds(pl.multiple_of(target * part, 16), part), :]
        for m in range(mb):
            raised = dot(up2, stacks[m])
            level = pert[m, pl.ds(target * lp, lp)].astype(F32).reshape(part, mw)
            total = level * raised if m == 0 else total + level * raised
        for t in range(qblocks):
            ls[t, k * part : (k + 1) * part] = total[:, t * LANES : (t + 1) * LANES]
        for r in range(mr):
            for t in range(qblocks):
                mids[
                    r, pl.ds(pl.multiple_of(target * lp, 8), lp), t * LANES : (t + 1) * LANES
                ] = ls[t, pl.ds(k * part + r, lp, stride=mr), :]
        if k > 0:
            send_sum(0, k)
    for b in range(1, blocks):
        for k in range(1, nm):
            send_sum(b, k)

    centre = 2 * mr
    zero_mid = jnp.zeros((mr, lp, mw), F32)
    for at, absent in ((1, first), (0, lat < 2), (3, last), (4, lat >= nl - 2)):
        @pl.when(absent)
        def _():
            midx[pl.ds(at * mr, mr)] = zero_mid

    @pl.when(first)
    def _():
        adjr[0] = zero_mid
        for row in range(h1):
            fld[row] = jnp.zeros((lp, fw), F32)
            co[row] = jnp.zeros((3, fw), F32)

    @pl.when(last)
    def _():
        adjr[1] = zero_mid
        for row in range(h1):
            fld[h1 + fr + row] = jnp.zeros((lp, fw), F32)
            co[h1 + fr + row] = jnp.zeros((3, fw), F32)

    def add_up(b):
        levels = slice(8 * b, 8 * b + 8)
        total = mids[:, mem_slice(mem, b), :]
        for k in range(1, nm):
            rs[b, k].wait_recv()
            total = total + rsr[k - 1, :, levels, :]
        midx[pl.ds(centre, mr), levels, :] = total
        items = []
        for place, step in enumerate((1, -1, 2, -2)):
            item = lat_copy(
                10 + 4 * b + place, step,
                midx.at[pl.ds(centre, mr), block_levels(b), :],
                midx.at[pl.ds(centre - step * mr, mr), block_levels(b), :],
            )
            start(item)
            pending.append(item)
            items.append(item)
        return items

    def make_rows(b, at, rows, base, unroll):
        levels = slice(8 * b, 8 * b + 8)

        def one(i):
            row = []
            shares = [
                jnp.broadcast_to(wt[i, r : r + 1, :], (8, LANES)) for r in range(3 * mr)
            ]
            for t in range(qblocks):
                lanes = slice(t * LANES, (t + 1) * LANES)
                value = shares[0] * midx[base, levels, lanes]
                for r in range(1, 3 * mr):
                    value = value + shares[r] * midx[base + r, levels, lanes]
                row.append(value)
            row = jnp.concatenate(row, axis=1)
            before = pltpu.roll(row, 1, 1)
            after = pltpu.roll(row, mw - 1, 1)
            fld[i, levels, 0:mw] = 0.375 * before + 0.625 * row
            fld[i, levels, mw : 2 * mw] = 0.125 * before + 0.875 * row
            fld[i, levels, 2 * mw : 3 * mw] = 0.875 * row + 0.125 * after
            fld[i, levels, 3 * mw : 4 * mw] = 0.625 * row + 0.375 * after

        def step(i, carry):
            for u in range(unroll):
                one(at + i * unroll + u)
            return carry

        lax.fori_loop(0, rows // unroll, step, 0)

    def one_pass(b, low, steps):
        levels = slice(8 * b, 8 * b + 8)

        def phases(row):
            return [fld[row, levels, p * mw : (p + 1) * mw] for p in range(4)]

        def coef(row, kind, p):
            return co[row, kind : kind + 1, p * mw : (p + 1) * mw]

        centre0 = phases(low)
        under = phases(low - 1)
        flux0 = [coef(low - 1, 0, p) * (centre0[p] - under[p]) for p in range(4)]

        def step(i, carry):
            now, below_flux = carry
            for u in range(UNROLL):
                row = low + i * UNROLL + u
                over = phases(row + 1)
                east = [coef(row, 1, p) * (now[p + 1] - now[p]) for p in range(3)]
                east.append(coef(row, 1, 3) * (pltpu.roll(now[0], mw - 1, 1) - now[3]))
                edge = coef(row, 2, 0) * (now[0] - pltpu.roll(now[3], 1, 1))
                west = [edge] + east[:3]
                north = [coef(row, 0, p) * (over[p] - now[p]) for p in range(4)]
                for p in range(4):
                    fld[row, levels, p * mw : (p + 1) * mw] = now[p] + (
                        (north[p] - below_flux[p]) + (east[p] - west[p])
                    )
                now, below_flux = over, north
            return now, below_flux

        lax.fori_loop(0, steps, step, (centre0, flux0))

    def smooth(b, margin):
        levels = slice(8 * b, 8 * b + 8)

        def body(p, carry):
            low = margin + 1 + p
            one_pass(b, low, lax.div(ext - 2 * low + UNROLL - 1, UNROLL))

            @pl.when(last)
            def _():
                fld[h1 + fr, levels, :] = jnp.zeros((8, fw), F32)

            return carry

        lax.fori_loop(0, PASSES, body, 0)

    def apply_weights(b):
        levels = slice(8 * b, 8 * b + 8)

        def apply_own(i, carry):
            for u in range(4):
                row = 4 * i + u
                fld[h1 + row, levels, :] = fld[h1 + row, levels, :] * wown[row, levels, :]
            return carry

        lax.fori_loop(0, fr // 4, apply_own, 0)

        @pl.when(jnp.logical_not(first))
        def _():
            for i in range(h2):
                at = h1 - h2 + i
                fld[at, levels, :] = fld[at, levels, :] * wrows[0, i, levels, :]

        @pl.when(jnp.logical_not(last))
        def _():
            for i in range(h2):
                at = h1 + fr + i
                fld[at, levels, :] = fld[at, levels, :] * wrows[1, i, levels, :]

    def transpose_rows(b):
        levels = slice(8 * b, 8 * b + 8)

        def narrow(step, carry):
            for u in range(4):
                i = 4 * step + u
                g = [fld[h1 + i, levels, p * mw : (p + 1) * mw] for p in range(4)]
                value = 0.625 * (g[0] + g[3]) + 0.875 * (g[1] + g[2])
                value = value + pltpu.roll(0.375 * g[0] + 0.125 * g[1], mw - 1, 1)
                blend[i, levels, :] = value + pltpu.roll(0.125 * g[2] + 0.375 * g[3], 1, 1)
            return carry

        lax.fori_loop(0, fr // 4, narrow, 0)

        def gather(r):
            shares = [
                jnp.broadcast_to(wt[h1 + f, r : r + 1, :], (8, LANES)) for f in range(fr)
            ]
            for t in range(qblocks):
                lanes = slice(t * LANES, (t + 1) * LANES)
                value = shares[0] * blend[0, levels, lanes]
                for f in range(1, fr):
                    value = value + shares[f] * blend[f, levels, lanes]
                contrib[r, levels, lanes] = value

        for r in list(range(mr)) + list(range(2 * mr, 3 * mr)):
            gather(r)
        items = []
        for place, step, at in ((0, 1, 2 * mr), (1, -1, 0)):
            item = lat_copy(
                10 + 4 * blocks + 2 * b + place, step,
                contrib.at[pl.ds(at, mr), block_levels(b), :],
                adjr.at[place, :, block_levels(b), :],
            )
            start(item)
            pending.append(item)
            items.append(item)
        for r in range(mr, 2 * mr):
            gather(r)
        return items

    ag = {}

    def share(b, items):
        levels = slice(8 * b, 8 * b + 8)
        for item in items:
            wait_recv(item)
        mine = mem_slice(mem, b)
        fa[:, mine, :] = contrib[pl.ds(mr, mr), levels, :] + (
            adjr[0, :, levels, :] + adjr[1, :, levels, :]
        )
        for k in range(1, nm):
            target = lax.rem(mem + k, nm)
            slot = 10 + 6 * blocks + ((blocks + b) * nm + k)
            copy = pltpu.make_async_remote_copy(
                src_ref=fa.at[:, mine, :], dst_ref=fa.at[:, mine, :],
                send_sem=send_sem.at[slot], recv_sem=recv_sem.at[slot],
                device_id={"mem": target}, device_id_type=MESH,
            )
            copy.start()
            ag[b, k] = copy

    near = {0: add_up(0)}
    start(w_up)
    start(w_dn)
    previous = None
    for b in range(blocks):
        if b == 0:
            wait_recv(s_up)
            wait_recv(s_dn)
        for item in near[b][:2]:
            wait_recv(item)
        make_rows(b, h1, fr, mr, 4)
        for item in near[b][2:]:
            wait_recv(item)

        @pl.when(jnp.logical_not(first))
        def _():
            make_rows(b, 0, h1, 0, 5)

        @pl.when(jnp.logical_not(last))
        def _():
            make_rows(b, h1 + fr, h1, 2 * mr, 5)

        if b + 1 < blocks:
            near[b + 1] = add_up(b + 1)
        if b == 0:
            wait_recv(k_up)
            wait_recv(k_dn)
        smooth(b, 0)
        if previous is not None:
            share(b - 1, previous)
        if b == 0:
            wait_recv(w_up)
            wait_recv(w_dn)
        apply_weights(b)
        smooth(b, PASSES)
        previous = transpose_rows(b)
    share(blocks - 1, previous)
    part = lp * mr
    for k in range(nm):
        source = lax.rem(mem + (nm - k), nm)
        if k > 0:
            for b in range(blocks):
                ag[b, k].wait_recv()
        for r in range(mr):
            for t in range(qblocks):
                ls[t, pl.ds(k * part + r, lp, stride=mr), :] = fa[
                    r, pl.ds(pl.multiple_of(source * lp, 8), lp), t * LANES : (t + 1) * LANES
                ]
        spread = jnp.concatenate(
            [ls[t, k * part : (k + 1) * part] for t in range(qblocks)], axis=1
        )
        down = down_ref[source]
        for m in range(mb):
            level = pert[m, pl.ds(source * lp, lp)].astype(F32).reshape(part, mw)
            value = dot(down, jnp.concatenate(split2(level * spread), axis=0))
            if k == 0:
                tall[m] = value
            else:
                tall[m] += value
    lont = lont_ref[...]
    for m in range(mb):
        thin = split2(tall[m])
        grad = dot(thin[0], lont) + dot(thin[1], lont)
        for c in range(3):
            gp[c, m] = grad[c * cl : (c + 1) * cl]
    g_up = lat_copy(8, 1, gp.at[2], gpr.at[0])
    g_dn = lat_copy(9, -1, gp.at[0], gpr.at[1])
    for item in (g_up, g_dn):
        start(item)
        pending.append(item)

    @pl.when(first)
    def _():
        gpr[0] = gp[0]

    @pl.when(last)
    def _():
        gpr[1] = gp[2]

    wait_recv(g_up)
    wait_recv(g_dn)
    out_ref[...] = ctl_ref[...] + (gp[1] + (gpr[0] + gpr[1]))
    for item in pending:
        wait_send(item)
    for copy in list(rs.values()) + list(ag.values()):
        copy.wait_send()


def body(controls, perturbations, precision_weight, north_coef, east_coef, fine_source, fine_frac):
    nm, nl = lax.axis_size("mem"), lax.axis_size("lat")
    mb, cl, _, cw = controls.shape
    _, lv, mr, mw = perturbations.shape
    fr, fw = north_coef.shape
    lp = lv // nm
    h1, h2 = 2 * PASSES, PASSES
    ext = fr + 2 * h1
    level = refine_matrix(cl, "edge")
    across = refine_matrix(1, "pad")
    up = np.einsum("vc,ra->vrac", level, across).reshape(lv * mr, 3 * cl)
    down = up.T.reshape(3 * cl, nm, lp * mr).transpose(1, 0, 2)
    lon = refine_matrix(cw, "wrap").T
    vmem = pl.BlockSpec(memory_space=pltpu.VMEM)
    smem = pl.BlockSpec(memory_space=pltpu.SMEM)
    anywhere = pl.BlockSpec(memory_space=pl.ANY)
    dims = (nm, nl, mb, cl, cw, lv, mr, mw, fr, fw)
    blocks = lp // 8
    slots = 10 + 6 * blocks + 2 * blocks * nm
    taps = -(-3 * mr // 8) * 8
    result = pl.pallas_call(
        functools.partial(kernel, dims),
        out_shape=jax.ShapeDtypeStruct((mb, cl, cw), F32),
        in_specs=[vmem, anywhere, anywhere, vmem, vmem, smem, smem] + [vmem] * 4,
        out_specs=vmem,
        scratch_shapes=[
            pltpu.VMEM((2, mb, cl, cw), F32),
            pltpu.VMEM((mb, lv, mr, mw), BF16),
            pltpu.VMEM((lp, fr, fw), BF16),
            pltpu.VMEM((2, h2, lp, fw), F32),
            pltpu.VMEM((ext + UNROLL, 3, fw), F32),
            pltpu.VMEM((ext, taps, LANES), F32),
            pltpu.VMEM((mw // LANES, lv * mr, LANES), F32),
            pltpu.VMEM((mr, lv, mw), F32),
            pltpu.VMEM((nm - 1, mr, lp, mw), F32),
            pltpu.VMEM((5 * mr, lp, mw), F32),
            pltpu.VMEM((ext + UNROLL, lp, fw), F32),
            pltpu.VMEM((fr, lp, mw), F32),
            pltpu.VMEM((3 * mr, lp, mw), F32),
            pltpu.VMEM((2, mr, lp, mw), F32),
            pltpu.VMEM((mr, lv, mw), F32),
            pltpu.VMEM((3, mb, cl, cw), F32),
            pltpu.VMEM((2, mb, cl, cw), F32),
            pltpu.VMEM((fr, lp, fw), F32),
            pltpu.VMEM((mb, 3 * cl, mw), F32),
            pltpu.SemaphoreType.DMA((2,)),
            pltpu.SemaphoreType.DMA((slots,)),
            pltpu.SemaphoreType.DMA((slots,)),
        ],
        compiler_params=pltpu.CompilerParams(collective_id=0, has_side_effects=True),
    )(
        controls.reshape(mb, cl, cw),
        perturbations,
        precision_weight,
        north_coef,
        east_coef,
        fine_source,
        fine_frac,
        jnp.asarray(np.concatenate([up] * 2, axis=1), BF16),
        jnp.asarray(lon, BF16),
        jnp.asarray(np.concatenate([down] * 2, axis=2), BF16),
        jnp.asarray(lon.T, BF16),
    )
    return result.reshape(controls.shape)


def solution(mesh):
    in_specs = (
        P("mem", None, "lat", None),
        P("mem", None, "lat", None),
        P(None, "lat", None),
        P("lat", None),
        P("lat", None),
        P("lat"),
        P("lat"),
    )
    out_specs = P("mem", None, "lat", None)
    return jax.shard_map(body, mesh=mesh, in_specs=in_specs, out_specs=out_specs, check_vma=False)
```
